32 devices in a mesh: dp: 8 (over y, x, core), mp: 4 (over z).
Axes of the slice: x: 2, y: 2, z: 4, core: 2. Of those that a mesh axis runs over, the one named last changes fastest.
Arguments:
- tokens: bfloat16 [32768, 512], P(('dp', 'mp')), may hold values from -6 to 6
- qkv_weight: bfloat16 [512, 1536], replicated, may hold values from -0.25 to 0.25
- out_weight: bfloat16 [512, 512], replicated, may hold values from -2 to 2
- norm1_gain: float32 [512], replicated, may hold values from 0.1 to 1.9
- norm1_shift: float32 [512], replicated, may hold values from -3 to 3
- norm2_gain: float32 [512], replicated, may hold values from 0.1 to 1.9
- norm2_shift: float32 [512], replicated, may hold values from -3 to 3
- up_weight: bfloat16 [512, 2048], P(None, 'mp'), may hold values from -0.25 to 0.25
- up_bias: bfloat16 [2048], P('mp'), may hold values from -3 to 3
- down_weight: bfloat16 [2048, 512], P('mp'), may hold values from -0.125 to 0.125
- down_bias: float32 [512], replicated, may hold values from -3 to 3
- lengths: int32 [17], replicated, may hold values from 512 to 16384, as said below
- cotangent: bfloat16 [32768, 512], P(('dp', 'mp')), may hold values from -6 to 6
Outputs:
- output: bfloat16 [32768, 512], P(('dp', 'mp'))
- input_grad: bfloat16 [32768, 512], P(('dp', 'mp'))
- qkv_grad: float32 [512, 1536], replicated
- out_grad: float32 [512, 512], replicated
- norm1_gain_grad: float32 [512], replicated
- norm1_shift_grad: float32 [512], replicated
- norm2_gain_grad: float32 [512], replicated
- norm2_shift_grad: float32 [512], replicated
- up_grad: float32 [512, 2048], P(None, 'mp')
- up_bias_grad: float32 [2048], P('mp')
- down_grad: float32 [2048, 512], P('mp')
- down_bias_grad: float32 [512], replicated
The draws below stay inside these ranges and needn't reach their ends.
Inputs may be any that keep to these rules, and one draw needn't show every extreme that they name: The 17 lengths add up to 32768; 1 of them equal 16384, and the others lie between 512 and 1536, both ends reached.
All inputs are finite; a program needn't handle non-finite values.
Results may differ from the reference program's by a relative error of at most 0.012.
Values may be sent and summed in bfloat16 or wider, within the bound.
No kernel may reach another device: no remote copies, remote signals or barrier semaphores. Data moves between devices by JAX's collectives and lax.ppermute only.
A program may use at most 192 MiB of HBM per device.

```python
import jax
import jax.numpy as jnp
from jax import lax

HEADS = 8
HEAD_DIM = 64
D = 512
FF = 2048
BLK = 512
LONG_LEN = 16384
SHORT_LEN = 1024
TOKENS = 32768
NLONG = 1
NSHORT = 16


def draw_lengths(key, part):
    pair_key = jax.random.fold_in(key, 11)
    order_key = jax.random.fold_in(key, 23)
    halves = jax.random.randint(pair_key, (NSHORT // 2,), SHORT_LEN // 2, 3 * SHORT_LEN // 2 + 1).astype(jnp.int32)
    halves = halves.at[0].set(SHORT_LEN // 2)
    shorts = jnp.stack([halves, 2 * SHORT_LEN - halves], axis=1).reshape(-1).astype(jnp.int32)
    longs = jnp.full((NLONG,), LONG_LEN, jnp.int32)
    joined = jnp.concatenate([longs, shorts])
    ordering = jax.random.permutation(order_key, NLONG + NSHORT)
    return joined[ordering].astype(jnp.int32)


def steps_of(stream_key, extent, cuts, low, high):
    factor_of = 1.0
    for axis_at, parts in cuts:
        heights = jax.random.uniform(jax.random.fold_in(jax.random.fold_in(stream_key, 6), axis_at), (parts,), jnp.float32, low / len(cuts), high / len(cuts))
        factor_of = factor_of * jnp.repeat(jnp.exp(heights), extent[axis_at] // parts).reshape((-1,) + (1,) * (len(extent) - 1 - axis_at))
    return factor_of


def noise(rng, extent, scale, bound, cuts=(), kind=jnp.bfloat16):
    drawn = jax.random.normal(rng, extent, jnp.float32) * scale
    if len(cuts) > 0:
        drawn = steps_of(rng, extent, cuts, -0.22, 0.18) * drawn
    return jnp.clip(drawn, min=-bound, max=bound).astype(kind)


def setup_inputs(seed: int = 0) -> dict:
    key_list = jax.random.split(jax.random.key(seed), 14)
    return {
        "tokens": noise(key_list[0], (TOKENS, D), 1.0, 6.0, ((0, 32),)),
        "qkv_weight": noise(key_list[1], (D, 3 * D), D ** -0.5, 0.25),
        "out_weight": noise(key_list[2], (D, D), (D // 64) ** -0.5, 2.0),
        "norm1_gain": jnp.clip(1.0 + 0.18 * jax.random.normal(key_list[3], (D,), jnp.float32), 0.1, 1.9),
        "norm1_shift": noise(key_list[4], (D,), 0.5, 3.0, (), jnp.float32),
        "norm2_gain": jnp.clip(1.0 + 0.18 * jax.random.normal(key_list[5], (D,), jnp.float32), 0.1, 1.9),
        "norm2_shift": noise(key_list[6], (D,), 0.5, 3.0, (), jnp.float32),
        "up_weight": noise(key_list[7], (D, FF), D ** -0.5, 0.25, ((1, 4),)),
        "up_bias": noise(key_list[8], (FF,), 0.5, 3.0, ((0, 4),)),
        "down_weight": noise(key_list[9], (FF, D), FF ** -0.5, 0.125, ((0, 4),)),
        "down_bias": noise(key_list[10], (D,), 0.5, 3.0, (), jnp.float32),
        "lengths": draw_lengths(jax.random.fold_in(key_list[13], 71), 0),
        "cotangent": noise(key_list[12], (TOKENS, D), 1.0, 6.0, ((0, 32),)),
    }


NORM_EPS = 1e-05
SCORE_EPS = 1e-06
EXACT_MODE = lax.Precision.HIGHEST

@jax.custom_vjp
def low(v):
    return lax.optimization_barrier(v.astype(jnp.bfloat16)).astype(jnp.float32)

@jax.custom_vjp
def low_back(v):
    return v

def low_keep(v):
    return (low(v), None)

def low_pass(kept, grad):
    return (grad,)

def back_keep(v):
    return (v, None)

def back_low(kept, grad):
    return (low(grad),)
low.defvjp(low_keep, low_pass)
low_back.defvjp(back_keep, back_low)

def normalize(rows, gain, shift):
    centred = rows - lax.optimization_barrier(jnp.mean(rows, axis=-1, keepdims=True))
    inv_std = lax.rsqrt(lax.optimization_barrier(jnp.mean(centred * centred, axis=-1, keepdims=True)) + NORM_EPS)
    return centred * inv_std * gain + shift

def segment_rows(lengths, count):
    ends = jnp.cumsum(lengths).astype(jnp.int32)
    starts = (ends - lengths).astype(jnp.int32)
    places = jnp.arange(count, dtype=jnp.int32)
    segment = lax.optimization_barrier(jnp.sum((ends[None, :] <= places[:, None]).astype(jnp.int32), axis=1)).astype(jnp.int32)
    opening = lax.optimization_barrier(jnp.sum((starts[None, :] == places[:, None]).astype(jnp.int32), axis=1)).astype(jnp.int32)
    return (segment, opening)

def attention(normed, qkv_weight, segment, opening):
    width = HEADS * HEAD_DIM

    def block_step(carry, index):
        state, total = carry
        start = index * BLK
        rows_in = lax.dynamic_slice_in_dim(normed, start, BLK, 0)
        block_seg = lax.dynamic_slice_in_dim(segment, start, BLK, 0)
        first_open = lax.dynamic_slice_in_dim(opening, start, 1, 0)[0]
        projected = low_back(jnp.dot(rows_in, qkv_weight, precision=EXACT_MODE))
        query = low(jax.nn.elu(projected[:, :width]) + 1.0).reshape(BLK, HEADS, HEAD_DIM)
        keys = low(jax.nn.elu(projected[:, width:2 * width]) + 1.0).reshape(BLK, HEADS, HEAD_DIM)
        values = low(projected[:, 2 * width:]).reshape(BLK, HEADS, HEAD_DIM)
        carried = ((block_seg == block_seg[0]) & (first_open == 0)).astype(jnp.float32)
        ending = (block_seg == block_seg[-1]).astype(jnp.float32)
        places = jnp.arange(BLK, dtype=jnp.int32)
        allowed = ((places[None, :] <= places[:, None]) & (block_seg[None, :] == block_seg[:, None])).astype(jnp.float32)
        scores = jnp.einsum('ihd,jhd->hij', query, keys, precision=EXACT_MODE)
        masked = low_back(scores * allowed[None])
        weights = low(masked)
        numerator = jnp.einsum('hij,jhd->ihd', weights, values, precision=EXACT_MODE)
        numerator = numerator + carried[:, None, None] * jnp.einsum('ihd,hde->ihe', query, state, precision=EXACT_MODE)
        numerator = low_back(numerator)
        denominator = lax.optimization_barrier(jnp.sum(masked, axis=-1)).T + carried[:, None] * jnp.einsum('ihd,hd->ih', query, total, precision=EXACT_MODE) + SCORE_EPS
        context = low_back(numerator / denominator[:, :, None])
        keep = carried[-1]
        key_end = keys * ending[:, None, None]
        new_state = keep * state + jnp.einsum('jhd,jhe->hde', key_end, values, precision=EXACT_MODE)
        new_total = keep * total + lax.optimization_barrier(jnp.sum(key_end, axis=0))
        return ((new_state, new_total), low(context).reshape(BLK, width))
    initial = (jnp.zeros((HEADS, HEAD_DIM, HEAD_DIM), jnp.float32), jnp.zeros((HEADS, HEAD_DIM), jnp.float32))
    _, pieces = lax.scan(jax.checkpoint(block_step), initial, jnp.arange(TOKENS // BLK, dtype=jnp.int32))
    return pieces.reshape(TOKENS, width)

def reference(tokens, qkv_weight, out_weight, norm1_gain, norm1_shift, norm2_gain, norm2_shift, up_weight, up_bias, down_weight, down_bias, lengths, cotangent):
    segment, opening = segment_rows(lengths, TOKENS)

    def forward(inputs, qkv_full, out_full, gain_one, shift_one, gain_two, shift_two, up_full, up_offset, down_full, down_offset):
        normed = low(normalize(inputs, gain_one, shift_one))
        context = attention(normed, qkv_full, segment, opening)
        attended = low_back(jnp.dot(context, out_full, precision=EXACT_MODE))
        residual = inputs + attended
        second = low(normalize(residual, gain_two, shift_two))
        hidden_in = low_back(jnp.dot(second, up_full, precision=EXACT_MODE) + up_offset)
        hidden_low = low(jax.nn.gelu(hidden_in, approximate=False))
        return residual + jnp.dot(hidden_low, down_full, precision=EXACT_MODE) + down_offset
    output, pullback = jax.vjp(forward, tokens.astype(jnp.float32), qkv_weight.astype(jnp.float32), out_weight.astype(jnp.float32), norm1_gain.astype(jnp.float32), norm1_shift.astype(jnp.float32), norm2_gain.astype(jnp.float32), norm2_shift.astype(jnp.float32), up_weight.astype(jnp.float32), up_bias.astype(jnp.float32), down_weight.astype(jnp.float32), down_bias.astype(jnp.float32))
    grads = pullback(cotangent.astype(jnp.float32))
    return (output.astype(jnp.bfloat16), grads[0].astype(jnp.bfloat16), grads[1], grads[2], grads[3], grads[4], grads[5], grads[6], grads[7], grads[8], grads[9], grads[10])
```

```python
import functools

import jax
import jax.numpy as jnp
from jax import lax
from jax.experimental import pallas as pl
from jax.experimental.pallas import tpu as pltpu
from jax.sharding import PartitionSpec as P

HEADS = 8
HEAD_DIM = 64
PAIRS = HEADS // 2
LANES = 2 * HEAD_DIM
WIDTH = HEADS * HEAD_DIM
CHUNK = 256
NORM_EPS = 1e-05
SCORE_EPS = 1e-06
BF = jnp.bfloat16
F32 = jnp.float32
PACK = PAIRS * HEAD_DIM
PAYLOAD = PACK + 16


def dot(a, b):
    return lax.dot_general(a, b, (((1,), (0,)), ((), ())), preferred_element_type=F32)


def dot_t(a, b):
    return lax.dot_general(a, b, (((1,), (1,)), ((), ())), preferred_element_type=F32)


def t_dot(a, b):
    return lax.dot_general(a, b, (((0,), (0,)), ((), ())), preferred_element_type=F32)


def iota(shape, dim):
    return lax.broadcasted_iota(jnp.int32, shape, dim)


def count(flags, axis):
    return jnp.sum(flags.astype(F32), axis=axis, keepdims=True)


def seg_col(ends_row, first, size):
    shape = (size, ends_row.shape[1])
    return count(jnp.broadcast_to(ends_row, shape) <= first + iota(shape, 0), 1)


def seg_row(ends_col, first, size):
    shape = (ends_col.shape[0], size)
    return count(jnp.broadcast_to(ends_col, shape) <= first + iota(shape, 1), 0)


def seg_at(ends_row, place):
    return count(ends_row <= place, 1)


def not_open(ends_row, place):
    opens = count(ends_row == place, 1) + jnp.where(place == 0, 1.0, 0.0)
    return (opens == 0.0).astype(F32)


def block_diagonal():
    return (iota((LANES, LANES), 0) // HEAD_DIM == iota((LANES, LANES), 1) // HEAD_DIM).astype(F32)


def lane_masks(dtype):
    low = iota((1, LANES), 1) < HEAD_DIM
    return low.astype(F32).astype(dtype), (1.0 - low.astype(F32)).astype(dtype)


def pack_pair(full):
    low, high = lane_masks(F32)
    return full[:HEAD_DIM] * low + full[HEAD_DIM:] * high


def unpack_pair(packed, diagonal):
    return jnp.concatenate([packed, packed], axis=0) * diagonal


def column_of(row):
    high = row.astype(BF).astype(F32)
    rest = row - high
    at = iota((16, LANES), 0)
    rows = jnp.where(at == 0, high, 0.0) + jnp.where(at == 1, rest, 0.0)
    return t_dot(rows.astype(BF), jnp.ones((16, LANES), BF))


def pair_slice(p):
    return slice(p * LANES, (p + 1) * LANES)


def head_sums(values):
    ones = block_diagonal().astype(BF)
    out = []
    for p in range(PAIRS):
        v = values[:, pair_slice(p)]
        high = v.astype(BF)
        rest = (v - high.astype(F32)).astype(BF)
        out.append(dot(high, ones) + dot(rest, ones))
    return jnp.concatenate(out, axis=1)


def normalize(rows, gain, shift):
    centred = rows - jnp.mean(rows, axis=-1, keepdims=True)
    inv_std = lax.rsqrt(jnp.mean(centred * centred, axis=-1, keepdims=True) + NORM_EPS)
    scaled = centred * inv_std
    return scaled * gain + shift, scaled, inv_std


def normalize_back(upstream, scaled, inv_std, gain):
    weighted = upstream * gain
    centred = weighted - jnp.mean(weighted, axis=-1, keepdims=True)
    inner = centred - scaled * jnp.mean(weighted * scaled, axis=-1, keepdims=True)
    return inner * inv_std


def normal_parts(v):
    bell = jnp.exp(-0.5 * v * v)
    z = jnp.abs(v) * 0.7071067811865476
    t = 1.0 / (1.0 + 0.3275911 * z)
    poly = t * (
        0.254829592
        + t * (-0.284496736 + t * (1.421413741 + t * (-1.453152027 + t * 1.061405429)))
    )
    half = 0.5 * poly * bell
    return jnp.where(v >= 0.0, 1.0 - half, half), bell


def total_rows(state, total):
    rows = [state]
    rows += [total[:, pair_slice(p)] for p in range(PAIRS)]
    rows.append(jnp.zeros((PAYLOAD - PACK - PAIRS, LANES), F32))
    return jnp.concatenate(rows, axis=0)


def forward_kernel(
    first_ref,
    x_ref,
    w_ref,
    gain_ref,
    shift_ref,
    ends_row_ref,
    ends_col_ref,
    normed_ref,
    feat_ref,
    num_ref,
    den_ref,
    states_ref,
    totals_ref,
    end_ref,
    state,
    total,
):
    b = pl.program_id(0)

    @pl.when(b == 0)
    def _():
        state[...] = jnp.zeros_like(state)
        total[...] = jnp.zeros_like(total)

    first = first_ref[0] + b * CHUNK
    ends_row = ends_row_ref[...]
    seg_c = seg_col(ends_row, first, CHUNK)
    seg_r = seg_row(ends_col_ref[...], first, CHUNK)
    seg_first = seg_r[:, :1]
    seg_last = seg_r[:, CHUNK - 1 :]
    flow = not_open(ends_row, first)
    carried = (seg_c == seg_first).astype(F32) * flow
    ending = (seg_c == seg_last).astype(F32)
    keep = (seg_first == seg_last).astype(F32) * flow
    square = (CHUNK, CHUNK)
    allowed = jnp.where(
        (iota(square, 1) <= iota(square, 0)) & (seg_c == seg_r), 1.0, 0.0
    )

    x = x_ref[...].astype(F32)
    normed, _, _ = normalize(x, gain_ref[...], shift_ref[...])
    low = normed.astype(BF)
    normed_ref[...] = low
    projected = dot(low, w_ref[...])
    raw = projected[:, : 2 * WIDTH]
    phi = jnp.where(raw > 0.0, raw + 1.0, jnp.exp(jnp.minimum(raw, 0.0)))
    query = phi[:, :WIDTH].astype(BF)
    keys = phi[:, WIDTH:].astype(BF)
    values = projected[:, 2 * WIDTH :].astype(BF)
    feat_ref[:, :WIDTH] = query
    feat_ref[:, WIDTH : 2 * WIDTH] = keys
    feat_ref[:, 2 * WIDTH :] = values

    diagonal = block_diagonal()
    masks = lane_masks(BF)
    totals_ref[0] = total[...]
    carried_low = carried.astype(BF)
    ending_low = ending.astype(BF)
    for p in range(PAIRS):
        s = pair_slice(p)
        q, k, v = query[:, s], keys[:, s], values[:, s]
        weights, sides = [], []
        for m in masks:
            scores = dot_t(q, k * m) * allowed
            weights.append(scores.astype(BF))
            sides.append(
                jnp.concatenate([v * m, jnp.broadcast_to(m, (CHUNK, LANES))], axis=1)
            )
        packed = state[p]
        states_ref[0, p * HEAD_DIM : (p + 1) * HEAD_DIM, :] = packed
        row = total[0:1, s]
        before = jnp.concatenate(
            [unpack_pair(packed, diagonal), column_of(row) * diagonal], axis=1
        ).astype(BF)
        both = dot(
            jnp.concatenate(weights, axis=1), jnp.concatenate(sides, axis=0)
        ) + dot(q * carried_low, before)
        num_ref[:, s] = both[:, :LANES]
        den_ref[:, s] = both[:, LANES:]
        k_end = k * ending_low
        state[p] = keep * packed + pack_pair(t_dot(k_end, v))
        total[0:1, s] = keep * row + jnp.sum(k_end.astype(F32), axis=0, keepdims=True)

    @pl.when(b == pl.num_programs(0) - 1)
    def _():
        end_ref[...] = total_rows(
            jnp.concatenate([state[p] for p in range(PAIRS)], axis=0), total[0:1, :]
        ).astype(BF)


def middle_kernel(
    first_ref,
    x_ref,
    query_ref,
    num_ref,
    den_ref,
    prior_ref,
    out_w_ref,
    gain_ref,
    shift_ref,
    up_ref,
    up_bias_ref,
    down_ref,
    down_bias_ref,
    g_ref,
    ends_row_ref,
    output_ref,
    residual_grad_ref,
    second_ref,
    hidden_ref,
    hidden_grad_ref,
    context_ref,
    attended_grad_ref,
    numer_grad_ref,
    denom_grad_ref,
    vectors_ref,
    bias_grad_ref,
    end_ref,
    state,
    total,
):
    b = pl.program_id(0)
    shards = up_ref.shape[0]

    @pl.when(b == 0)
    def _():
        state[...] = jnp.zeros_like(state)
        total[...] = jnp.zeros_like(total)
        vectors_ref[...] = jnp.zeros_like(vectors_ref)
        bias_grad_ref[...] = jnp.zeros_like(bias_grad_ref)

    ends_row = ends_row_ref[...]
    own = first_ref[0]
    seg_c = seg_col(ends_row, own + b * CHUNK, CHUNK)
    cont = (seg_c == seg_at(ends_row, own)).astype(F32) * not_open(ends_row, own)
    cont_low = cont.astype(BF)
    diagonal = block_diagonal()
    query = query_ref[...]
    numer, denom = [], []
    for p in range(PAIRS):
        s = pair_slice(p)
        packed = prior_ref[p * HEAD_DIM : (p + 1) * HEAD_DIM, :]
        row = prior_ref[PACK + p : PACK + p + 1, :]
        before = jnp.concatenate(
            [unpack_pair(packed, diagonal), column_of(row) * diagonal], axis=1
        ).astype(BF)
        both = dot(query[:, s] * cont_low, before)
        numer.append(both[:, :LANES])
        denom.append(both[:, LANES:])
    numer = num_ref[...] + jnp.concatenate(numer, axis=1)
    inv_den = 1.0 / (den_ref[...] + jnp.concatenate(denom, axis=1) + SCORE_EPS)
    context = numer * inv_den
    context_low = context.astype(BF)
    context_ref[...] = context_low
    residual = x_ref[...].astype(F32) + dot(context_low, out_w_ref[...])
    gain = gain_ref[...]
    normed, scaled, inv_std = normalize(residual, gain, shift_ref[...])
    second = normed.astype(BF)
    second_ref[...] = second
    g = g_ref[...]
    g_wide = g.astype(F32)
    fed = jnp.zeros((CHUNK, WIDTH), F32)
    second_grad = jnp.zeros((CHUNK, WIDTH), F32)
    for j in range(shards):
        hidden_in = dot(second, up_ref[j]) + up_bias_ref[j : j + 1, :].astype(F32)
        phi, bell = normal_parts(hidden_in)
        hidden = (hidden_in * phi).astype(BF)
        hidden_ref[j] = hidden
        fed = fed + dot(hidden, down_ref[j])
        slope = phi + hidden_in * bell * 0.3989422804014327
        hidden_grad = (dot_t(g, down_ref[j]) * slope).astype(BF)
        hidden_grad_ref[j] = hidden_grad
        bias_grad_ref[j : j + 1, :] += jnp.sum(hidden_grad.astype(F32), axis=0, keepdims=True)
        second_grad = second_grad + dot_t(hidden_grad, up_ref[j])
    output_ref[...] = (residual + fed + down_bias_ref[...]).astype(BF)
    vectors_ref[0:1, :] += jnp.sum(second_grad * scaled, axis=0, keepdims=True)
    vectors_ref[1:2, :] += jnp.sum(second_grad, axis=0, keepdims=True)
    vectors_ref[2:3, :] += jnp.sum(g_wide, axis=0, keepdims=True)
    residual_grad = g_wide + normalize_back(second_grad, scaled, inv_std, gain)
    residual_grad_ref[...] = residual_grad
    attended_grad = residual_grad.astype(BF)
    attended_grad_ref[...] = attended_grad
    context_grad = dot_t(attended_grad, out_w_ref[...]).astype(BF).astype(F32)
    numer_grad = (context_grad * inv_den).astype(BF)
    numer_grad_ref[...] = numer_grad
    denom_grad = -head_sums(context_grad * context) * inv_den
    denom_grad_ref[...] = denom_grad
    reach = query * cont_low
    for p in range(PAIRS):
        s = pair_slice(p)
        state[p] += pack_pair(t_dot(reach[:, s], numer_grad[:, s]))
    total[0:1, :] += jnp.sum(reach.astype(F32) * denom_grad, axis=0, keepdims=True)

    @pl.when(b == pl.num_programs(0) - 1)
    def _():
        end_ref[...] = total_rows(
            jnp.concatenate([state[p] for p in range(PAIRS)], axis=0), total[0:1, :]
        ).astype(BF)


def backward_kernel(
    first_ref,
    feat_ref,
    numer_grad_ref,
    denom_grad_ref,
    states_ref,
    totals_ref,
    prior_ref,
    ends_row_ref,
    ends_col_ref,
    grads_ref,
    state,
    total,
):
    step = pl.program_id(0)
    b = pl.num_programs(0) - 1 - step

    @pl.when(step == 0)
    def _():
        state[...] = jnp.zeros_like(state)
        total[...] = jnp.zeros_like(total)

    own = first_ref[0]
    first = own + b * CHUNK
    ends_row = ends_row_ref[...]
    seg_c = seg_col(ends_row, first, CHUNK)
    seg_r = seg_row(ends_col_ref[...], first, CHUNK)
    seg_first = seg_r[:, :1]
    seg_last = seg_r[:, CHUNK - 1 :]
    flow = not_open(ends_row, first)
    carried = (seg_c == seg_first).astype(F32) * flow
    ending = (seg_c == seg_last).astype(F32)
    keep = (seg_first == seg_last).astype(F32) * flow
    prior = (seg_first == seg_at(ends_row, own)).astype(F32) * not_open(ends_row, own)
    square = (CHUNK, CHUNK)
    allowed = jnp.where(
        (iota(square, 1) <= iota(square, 0)) & (seg_c == seg_r), 1.0, 0.0
    )
    diagonal = block_diagonal()
    masks = lane_masks(BF)
    carried_low = carried.astype(BF)
    lane = iota((1, LANES), 1)
    upper = lane % HEAD_DIM < HEAD_DIM // 2
    for p in range(PAIRS):
        s = pair_slice(p)
        q = feat_ref[:, s]
        k = feat_ref[:, WIDTH + p * LANES : WIDTH + (p + 1) * LANES]
        v = feat_ref[:, 2 * WIDTH + p * LANES : 2 * WIDTH + (p + 1) * LANES]
        ng = numer_grad_ref[:, s]
        dg = denom_grad_ref[:, s]
        dg_high = dg.astype(BF).astype(F32)
        dg_parts = jnp.where(upper, dg_high, dg - dg_high).astype(BF)
        left = jnp.concatenate([ng, dg_parts], axis=1)
        pair_grads, keys, key_grad, value_grad = [], [], 0.0, 0.0
        for h, m in enumerate(masks):
            k_own = k * m
            keys.append(k_own)
            weights = (dot_t(q, k_own) * allowed).astype(BF)
            pick = (lane == h * HEAD_DIM) | (lane == h * HEAD_DIM + HEAD_DIM // 2)
            pick = jnp.where(pick, 1.0, 0.0).astype(BF)
            right = jnp.concatenate(
                [v * m, jnp.broadcast_to(pick, (CHUNK, LANES))], axis=1
            )
            pair_grad = (dot_t(left, right) * allowed).astype(BF)
            pair_grads.append(pair_grad)
            key_grad = key_grad + t_dot(pair_grad, q * m)
            value_grad = value_grad + t_dot(weights, ng * m)
        rows = slice(p * HEAD_DIM, (p + 1) * HEAD_DIM)
        packed = states_ref[0, rows, :] + prior * prior_ref[rows, :]
        row = totals_ref[0, 0:1, s] + prior * prior_ref[PACK + p : PACK + p + 1, :]
        before = unpack_pair(packed, diagonal).astype(BF)
        query_grad = dot(
            jnp.concatenate(pair_grads, axis=1), jnp.concatenate(keys, axis=0)
        ) + carried * (dot_t(ng, before) + dg * row)
        after = state[p]
        after_row = total[0:1, s]
        after_low = unpack_pair(after, diagonal).astype(BF)
        key_grad = key_grad + ending * (dot_t(v, after_low) + after_row)
        value_grad = value_grad + ending * dot(k, after_low)
        grads_ref[:, s] = query_grad
        grads_ref[:, WIDTH + p * LANES : WIDTH + (p + 1) * LANES] = key_grad
        grads_ref[:, 2 * WIDTH + p * LANES : 2 * WIDTH + (p + 1) * LANES] = value_grad
        reach = q * carried_low
        state[p] = keep * after + pack_pair(t_dot(reach, ng))
        total[0:1, s] = keep * after_row + jnp.sum(
            reach.astype(F32) * dg, axis=0, keepdims=True
        )


def last_kernel(
    first_ref,
    x_ref,
    feat_ref,
    grads_ref,
    later_ref,
    w_ref,
    gain_ref,
    shift_ref,
    residual_grad_ref,
    ends_row_ref,
    projected_grad_ref,
    input_grad_ref,
    vectors_ref,
):
    b = pl.program_id(0)

    @pl.when(b == 0)
    def _():
        vectors_ref[...] = jnp.zeros_like(vectors_ref)

    ends_row = ends_row_ref[...]
    own = first_ref[0]
    span = pl.num_programs(0) * CHUNK
    seg_c = seg_col(ends_row, own + b * CHUNK, CHUNK)
    reached = (seg_c == seg_at(ends_row, own + span - 1)).astype(F32)
    diagonal = block_diagonal()
    for p in range(PAIRS):
        sq = pair_slice(p)
        sk = pair_slice(PAIRS + p)
        sv = pair_slice(2 * PAIRS + p)
        after = unpack_pair(
            later_ref[p * HEAD_DIM : (p + 1) * HEAD_DIM, :], diagonal
        ).astype(BF)
        after_row = later_ref[PACK + p : PACK + p + 1, :]
        k = feat_ref[:, sk]
        key_grad = grads_ref[:, sk] + reached * (dot_t(feat_ref[:, sv], after) + after_row)
        value_grad = grads_ref[:, sv] + reached * dot(k, after)
        q_slope = jnp.minimum(feat_ref[:, sq].astype(F32), 1.0)
        k_slope = jnp.minimum(k.astype(F32), 1.0)
        projected_grad_ref[:, sq] = (grads_ref[:, sq] * q_slope).astype(BF)
        projected_grad_ref[:, sk] = (key_grad * k_slope).astype(BF)
        projected_grad_ref[:, sv] = value_grad.astype(BF)
    first_grad = dot_t(projected_grad_ref[...], w_ref[...])
    gain = gain_ref[...]
    _, scaled, inv_std = normalize(x_ref[...].astype(F32), gain, shift_ref[...])
    vectors_ref[0:1, :] += jnp.sum(first_grad * scaled, axis=0, keepdims=True)
    vectors_ref[1:2, :] += jnp.sum(first_grad, axis=0, keepdims=True)
    input_grad_ref[...] = (
        residual_grad_ref[...] + normalize_back(first_grad, scaled, inv_std, gain)
    ).astype(BF)


def call(kernel, steps, ins, outs, scratch=(), reverse=False):
    def spec(shape, dim, size):
        if dim is None:
            return pl.BlockSpec(shape, lambda i: (0,) * len(shape))
        block = shape[:dim] + (size,) + shape[dim + 1 :]

        def place(i):
            at = steps - 1 - i if reverse else i
            return tuple(at if d == dim else 0 for d in range(len(shape)))

        return pl.BlockSpec(block, place)

    in_specs = []
    for array, dim in ins:
        if dim == "scalar":
            in_specs.append(pl.BlockSpec(memory_space=pltpu.SMEM))
        else:
            size = None if dim is None else array.shape[dim] // steps
            in_specs.append(spec(array.shape, dim, size))
    out_specs = [
        spec(shape, dim, None if dim is None else shape[dim] // steps) for shape, _, dim in outs
    ]
    return pl.pallas_call(
        kernel,
        grid=(steps,),
        in_specs=in_specs,
        out_specs=out_specs,
        out_shape=[jax.ShapeDtypeStruct(shape, dtype) for shape, dtype, _ in outs],
        scratch_shapes=list(scratch),
        compiler_params=pltpu.CompilerParams(vmem_limit_bytes=56 * 1024 * 1024),
        name=kernel.__name__,
    )(*[array for array, _ in ins])


def shift(array, axis, by):
    n = lax.axis_size(axis)
    return lax.ppermute(array, axis, [(i, (i + by) % n) for i in range(n)])


def swap(array, axis, bit):
    n = lax.axis_size(axis)
    return lax.ppermute(array, axis, [(i, i ^ bit) for i in range(n)])


def bits_of(n):
    return [1 << i for i in range(n.bit_length() - 1)]


def bit_set(axis, bit):
    return (lax.axis_index(axis) // bit) % 2


def half(array, dim, which):
    size = array.shape[dim] // 2
    return lax.dynamic_slice_in_dim(array, which * size, size, dim)


def scatter_sum(array, axis, bits, dim):
    for bit in bits:
        mine = bit_set(axis, bit)
        sent = swap(half(array, dim, 1 - mine).astype(BF), axis, bit)
        array = half(array, dim, mine) + sent.astype(F32)
    return array


def gather_halves(array, axis, bits, dim):
    for bit in reversed(bits):
        other = swap(array, axis, bit)
        array = jnp.where(
            bit_set(axis, bit) == 0,
            jnp.concatenate([array, other], axis=dim),
            jnp.concatenate([other, array], axis=dim),
        )
    return array


def exchange(payload, weights_of):
    n_mp = lax.axis_size("mp")
    z = lax.axis_index("mp")
    near = [payload] + [shift(payload, "mp", k) for k in range(1, n_mp)]
    return near, z


def orders(n):
    bits = bits_of(n)
    if len(bits) < 3:
        return bits, bits
    return bits, bits[:1] + bits[2:] + bits[1:2]


def local(
    tokens,
    qkv_weight,
    out_weight,
    norm1_gain,
    norm1_shift,
    norm2_gain,
    norm2_shift,
    up_weight,
    up_bias,
    down_weight,
    down_bias,
    lengths,
    cotangent,
):
    rows, width = tokens.shape
    steps = rows // CHUNK
    n_dp, n_mp = lax.axis_size("dp"), lax.axis_size("mp")
    g_at, z_at = lax.axis_index("dp"), lax.axis_index("mp")
    me = g_at * n_mp + z_at
    first = (me * rows).astype(jnp.int32).reshape(1)
    n_seq = lengths.shape[0]
    order = jnp.arange(n_seq)
    ends = jnp.sum(jnp.where(order[:, None] >= order[None, :], lengths[None, :], 0), axis=1)
    ends_row = ends.reshape(1, n_seq).astype(jnp.int32)
    ends_col = ends.reshape(n_seq, 1).astype(jnp.int32)
    rows_of = lambda v: v.reshape(1, -1)

    shard = up_weight.shape[1]
    odd = bit_set("dp", 1)
    sent = jnp.where(odd == 0, up_weight, down_weight)
    halves = [shift(sent, "mp", k) for k in range(1, n_mp)]
    biases = [shift(up_bias, "mp", k) for k in range(1, n_mp)]
    others = [swap(h, "dp", 1) for h in halves]
    ups = jnp.stack([up_weight] + [jnp.where(odd == 0, a, b) for a, b in zip(halves, others)])
    downs = jnp.stack([down_weight] + [jnp.where(odd == 0, b, a) for a, b in zip(halves, others)])
    bias_all = jnp.stack([up_bias] + biases)

    scratch = [pltpu.VMEM((PAIRS, HEAD_DIM, LANES), F32), pltpu.VMEM((8, WIDTH), F32)]
    gain1, shift1 = rows_of(norm1_gain), rows_of(norm1_shift)
    normed_low, feat, numer, denom, states, totals, end_state = call(
        forward_kernel,
        steps,
        [
            (first, "scalar"),
            (tokens, 0),
            (qkv_weight, None),
            (gain1, None),
            (shift1, None),
            (ends_row, None),
            (ends_col, None),
        ],
        [
            ((rows, width), BF, 0),
            ((rows, 3 * width), BF, 0),
            ((rows, width), F32, 0),
            ((rows, width), F32, 0),
            ((steps, PACK, LANES), F32, 0),
            ((steps, 8, width), F32, 0),
            ((PAYLOAD, LANES), BF, None),
        ],
        scratch,
    )

    devices = n_dp * n_mp
    places = jnp.arange(devices, dtype=jnp.int32) * rows
    seg_firsts = jnp.sum((ends[None, :] <= places[:, None]).astype(jnp.int32), axis=1)
    seg_lasts = jnp.sum((ends[None, :] <= places[:, None] + (rows - 1)).astype(jnp.int32), axis=1)
    my_first = jnp.sum((ends <= first[0]).astype(jnp.int32))
    my_last = jnp.sum((ends <= first[0] + (rows - 1)).astype(jnp.int32))
    ids = jnp.arange(devices)
    from_before = ((ids < me) & (seg_lasts == my_first)).astype(F32).reshape(n_dp, n_mp)
    from_after = ((ids > me) & (seg_firsts == my_last)).astype(F32).reshape(n_dp, n_mp)

    def gather_states(payload):
        near = lax.all_gather(payload, "mp")
        return lax.all_gather(near, "dp")

    def weighted(everything, weights):
        return jnp.einsum("gz,gzrl->rl", weights, everything.astype(F32), precision="highest")

    prior = weighted(gather_states(end_state), from_before)

    gain2, shift2 = rows_of(norm2_gain), rows_of(norm2_shift)
    (
        output,
        residual_grad,
        second,
        hidden,
        hidden_grad,
        context_low,
        attended_grad,
        numer_grad,
        denom_grad,
        vectors2,
        bias_grad,
        end_grad,
    ) = call(
        middle_kernel,
        steps,
        [
            (first, "scalar"),
            (tokens, 0),
            (feat[:, :width], 0),
            (numer, 0),
            (denom, 0),
            (prior, None),
            (out_weight, None),
            (gain2, None),
            (shift2, None),
            (ups, None),
            (bias_all, None),
            (downs, None),
            (rows_of(down_bias), None),
            (cotangent, 0),
            (ends_row, None),
        ],
        [
            ((rows, width), BF, 0),
            ((rows, width), F32, 0),
            ((rows, width), BF, 0),
            ((n_mp, rows, shard), BF, 1),
            ((n_mp, rows, shard), BF, 1),
            ((rows, width), BF, 0),
            ((rows, width), BF, 0),
            ((rows, width), BF, 0),
            ((rows, width), F32, 0),
            ((8, width), F32, None),
            ((n_mp, shard), F32, None),
            ((PAYLOAD, LANES), BF, None),
        ],
        scratch,
    )
    later = weighted(gather_states(end_grad), from_after)

    up_pieces = jnp.einsum("td,jtf->jdf", second, hidden_grad, preferred_element_type=F32)
    down_pieces = jnp.einsum("jtf,td->jfd", hidden, cotangent, preferred_element_type=F32)
    order_a, order_b = orders(n_dp)

    def reduce_ffn(pieces, bits):
        part = scatter_sum(pieces, "dp", bits, 1)
        own = part[0]
        for k in range(1, n_mp):
            own = own + shift(part[k].astype(BF), "mp", -k).astype(F32)
        return gather_halves(own.astype(BF), "dp", bits, 0).astype(F32)

    grad_up = reduce_ffn(up_pieces, order_a)
    grad_down = reduce_ffn(down_pieces, order_b)

    (grads,) = call(
        backward_kernel,
        steps,
        [
            (first, "scalar"),
            (feat, 0),
            (numer_grad, 0),
            (denom_grad, 0),
            (states, 0),
            (totals, 0),
            (prior, None),
            (ends_row, None),
            (ends_col, None),
        ],
        [((rows, 3 * width), F32, 0)],
        scratch,
        reverse=True,
    )
    projected_grad, input_grad, vectors1 = call(
        last_kernel,
        steps,
        [
            (first, "scalar"),
            (tokens, 0),
            (feat, 0),
            (grads, 0),
            (later, None),
            (qkv_weight, None),
            (gain1, None),
            (shift1, None),
            (residual_grad, 0),
            (ends_row, None),
        ],
        [
            ((rows, 3 * width), BF, 0),
            ((rows, width), BF, 0),
            ((8, width), F32, None),
        ],
    )
    grad_qkv = jnp.einsum("td,tk->dk", normed_low, projected_grad, preferred_element_type=F32)
    grad_out = jnp.einsum("ti,to->io", context_low, attended_grad, preferred_element_type=F32)

    def reduce_all(part, bits):
        part = scatter_sum(part, "dp", bits, 0)
        size = part.shape[0] // n_mp
        cut = lambda k: lax.dynamic_slice_in_dim(part, ((z_at + k) % n_mp) * size, size, 0)
        own = cut(0)
        for k in range(1, n_mp):
            own = own + shift(cut(k).astype(BF), "mp", k).astype(F32)
        own = own.astype(BF)
        whole = jnp.zeros((n_mp, size, part.shape[1]), BF)
        whole = lax.dynamic_update_slice_in_dim(whole, own[None], z_at, 0)
        for k in range(1, n_mp):
            whole = lax.dynamic_update_slice_in_dim(
                whole, shift(own, "mp", k)[None], (z_at - k) % n_mp, 0
            )
        return gather_halves(whole.reshape(part.shape), "dp", bits, 0).astype(F32)

    grad_a = reduce_all(jnp.concatenate([grad_qkv[:, : 2 * width]], axis=1), order_a)
    grad_b = reduce_all(jnp.concatenate([grad_qkv[:, 2 * width :], grad_out], axis=1), order_b)

    vec = jnp.concatenate([vectors1[:2], vectors2[:3]], axis=0)
    for bit in bits_of(n_dp):
        both = swap(jnp.concatenate([vec, bias_grad.reshape(-1, width)]), "dp", bit)
        vec = vec + both[:5]
        bias_grad = bias_grad + both[5:].reshape(bias_grad.shape)
    for bit in bits_of(n_mp):
        vec = vec + swap(vec, "mp", bit)
    own_bias = bias_grad[0]
    for k in range(1, n_mp):
        own_bias = own_bias + shift(bias_grad[k], "mp", -k)

    return (
        output,
        input_grad,
        jnp.concatenate([grad_a, grad_b[:, :width]], axis=1),
        grad_b[:, width:],
        vec[0],
        vec[1],
        vec[2],
        vec[3],
        grad_up,
        own_bias,
        grad_down,
        vec[4],
    )


def solution(mesh):
    in_specs = (
        P(("dp", "mp"), None),
        P(),
        P(),
        P(),
        P(),
        P(),
        P(),
        P(None, "mp"),
        P("mp"),
        P("mp", None),
        P(),
        P(),
        P(("dp", "mp"), None),
    )
    out_specs = (
        P(("dp", "mp"), None),
        P(("dp", "mp"), None),
        P(),
        P(),
        P(),
        P(),
        P(),
        P(),
        P(None, "mp"),
        P("mp"),
        P("mp", None),
        P(),
    )
    return jax.shard_map(local, mesh=mesh, in_specs=in_specs, out_specs=out_specs, check_vma=False)
```

```python
import functools

import jax
import jax.numpy as jnp
from jax import lax
from jax.experimental import pallas as pl
from jax.experimental.pallas import tpu as pltpu
from jax.sharding import PartitionSpec as P

HEADS = 8
HEAD_DIM = 64
PAIRS = HEADS // 2
LANES = 2 * HEAD_DIM
WIDTH = HEADS * HEAD_DIM
CHUNK = 256
NORM_EPS = 1e-05
SCORE_EPS = 1e-06
BF = jnp.bfloat16
F32 = jnp.float32
PACK = PAIRS * HEAD_DIM
PAYLOAD = PACK + 16
BACK_CALLS = 4


def dot(a, b):
    return lax.dot_general(a, b, (((1,), (0,)), ((), ())), preferred_element_type=F32)


def dot_t(a, b):
    return lax.dot_general(a, b, (((1,), (1,)), ((), ())), preferred_element_type=F32)


def t_dot(a, b):
    return lax.dot_general(a, b, (((0,), (0,)), ((), ())), preferred_element_type=F32)


def iota(shape, dim):
    return lax.broadcasted_iota(jnp.int32, shape, dim)


def count(flags, axis):
    return jnp.sum(flags.astype(F32), axis=axis, keepdims=True)


def seg_col(ends_row, first, size):
    shape = (size, ends_row.shape[1])
    return count(jnp.broadcast_to(ends_row, shape) <= first + iota(shape, 0), 1)


def seg_row(ends_col, first, size):
    shape = (ends_col.shape[0], size)
    return count(jnp.broadcast_to(ends_col, shape) <= first + iota(shape, 1), 0)


def seg_at(ends_row, place):
    return count(ends_row <= place, 1)


def not_open(ends_row, place):
    opens = count(ends_row == place, 1) + jnp.where(place == 0, 1.0, 0.0)
    return (opens == 0.0).astype(F32)


def block_diagonal():
    return (iota((LANES, LANES), 0) // HEAD_DIM == iota((LANES, LANES), 1) // HEAD_DIM).astype(F32)


def lane_masks(dtype):
    low = iota((1, LANES), 1) < HEAD_DIM
    return low.astype(F32).astype(dtype), (1.0 - low.astype(F32)).astype(dtype)


def pack_pair(full):
    low, high = lane_masks(F32)
    return full[:HEAD_DIM] * low + full[HEAD_DIM:] * high


def unpack_pair(packed, diagonal):
    return jnp.concatenate([packed, packed], axis=0) * diagonal


def column_of(row):
    high = row.astype(BF).astype(F32)
    rest = row - high
    at = iota((16, LANES), 0)
    rows = jnp.where(at == 0, high, 0.0) + jnp.where(at == 1, rest, 0.0)
    return t_dot(rows.astype(BF), jnp.ones((16, LANES), BF))


def pair_slice(p):
    return slice(p * LANES, (p + 1) * LANES)


def head_sums(values):
    ones = block_diagonal().astype(BF)
    out = []
    for p in range(PAIRS):
        v = values[:, pair_slice(p)]
        high = v.astype(BF)
        rest = (v - high.astype(F32)).astype(BF)
        out.append(dot(high, ones) + dot(rest, ones))
    return jnp.concatenate(out, axis=1)


def normalize(rows, gain, shift):
    centred = rows - jnp.mean(rows, axis=-1, keepdims=True)
    inv_std = lax.rsqrt(jnp.mean(centred * centred, axis=-1, keepdims=True) + NORM_EPS)
    scaled = centred * inv_std
    return scaled * gain + shift, scaled, inv_std


def normalize_back(upstream, scaled, inv_std, gain):
    weighted = upstream * gain
    centred = weighted - jnp.mean(weighted, axis=-1, keepdims=True)
    inner = centred - scaled * jnp.mean(weighted * scaled, axis=-1, keepdims=True)
    return inner * inv_std


def normal_parts(v):
    bell = jnp.exp(-0.5 * v * v)
    z = jnp.abs(v) * 0.7071067811865476
    t = 1.0 / (1.0 + 0.3275911 * z)
    poly = t * (
        0.254829592
        + t * (-0.284496736 + t * (1.421413741 + t * (-1.453152027 + t * 1.061405429)))
    )
    half = 0.5 * poly * bell
    return jnp.where(v >= 0.0, 1.0 - half, half), bell


def total_rows(state, total):
    rows = [state]
    rows += [total[:, pair_slice(p)] for p in range(PAIRS)]
    rows.append(jnp.zeros((PAYLOAD - PACK - PAIRS, LANES), F32))
    return jnp.concatenate(rows, axis=0)


def forward_kernel(
    first_ref,
    x_ref,
    w_ref,
    gain_ref,
    shift_ref,
    ends_row_ref,
    ends_col_ref,
    normed_ref,
    feat_ref,
    num_ref,
    den_ref,
    states_ref,
    totals_ref,
    end_ref,
    state,
    total,
):
    b = pl.program_id(0)

    @pl.when(b == 0)
    def _():
        state[...] = jnp.zeros_like(state)
        total[...] = jnp.zeros_like(total)

    first = first_ref[0] + b * CHUNK
    ends_row = ends_row_ref[...]
    seg_c = seg_col(ends_row, first, CHUNK)
    seg_r = seg_row(ends_col_ref[...], first, CHUNK)
    seg_first = seg_r[:, :1]
    seg_last = seg_r[:, CHUNK - 1 :]
    flow = not_open(ends_row, first)
    carried = (seg_c == seg_first).astype(F32) * flow
    ending = (seg_c == seg_last).astype(F32)
    keep = (seg_first == seg_last).astype(F32) * flow
    square = (CHUNK, CHUNK)
    allowed = jnp.where(
        (iota(square, 1) <= iota(square, 0)) & (seg_c == seg_r), 1.0, 0.0
    )

    x = x_ref[...].astype(F32)
    normed, _, _ = normalize(x, gain_ref[...], shift_ref[...])
    low = normed.astype(BF)
    normed_ref[...] = low
    projected = dot(low, w_ref[...])
    raw = projected[:, : 2 * WIDTH]
    phi = jnp.where(raw > 0.0, raw + 1.0, jnp.exp(jnp.minimum(raw, 0.0)))
    query = phi[:, :WIDTH].astype(BF)
    keys = phi[:, WIDTH:].astype(BF)
    values = projected[:, 2 * WIDTH :].astype(BF)
    feat_ref[:, :WIDTH] = query
    feat_ref[:, WIDTH : 2 * WIDTH] = keys
    feat_ref[:, 2 * WIDTH :] = values

    diagonal = block_diagonal()
    masks = lane_masks(BF)
    totals_ref[0] = total[...]
    carried_low = carried.astype(BF)
    ending_low = ending.astype(BF)
    for p in range(PAIRS):
        s = pair_slice(p)
        q, k, v = query[:, s], keys[:, s], values[:, s]
        weights, sides = [], []
        for m in masks:
            scores = dot_t(q, k * m) * allowed
            weights.append(scores.astype(BF))
            sides.append(
                jnp.concatenate([v * m, jnp.broadcast_to(m, (CHUNK, LANES))], axis=1)
            )
        packed = state[p]
        states_ref[0, p * HEAD_DIM : (p + 1) * HEAD_DIM, :] = packed
        row = total[0:1, s]
        before = jnp.concatenate(
            [unpack_pair(packed, diagonal), column_of(row) * diagonal], axis=1
        ).astype(BF)
        both = dot(
            jnp.concatenate(weights, axis=1), jnp.concatenate(sides, axis=0)
        ) + dot(q * carried_low, before)
        num_ref[:, s] = both[:, :LANES]
        den_ref[:, s] = both[:, LANES:]
        k_end = k * ending_low
        state[p] = keep * packed + pack_pair(t_dot(k_end, v))
        total[0:1, s] = keep * row + jnp.sum(k_end.astype(F32), axis=0, keepdims=True)

    @pl.when(b == pl.num_programs(0) - 1)
    def _():
        end_ref[...] = total_rows(
            jnp.concatenate([state[p] for p in range(PAIRS)], axis=0), total[0:1, :]
        ).astype(BF)


def middle_kernel(
    first_ref,
    x_ref,
    query_ref,
    num_ref,
    den_ref,
    prior_ref,
    out_w_ref,
    gain_ref,
    shift_ref,
    up_ref,
    up_bias_ref,
    down_ref,
    down_bias_ref,
    odd_ref,
    g_ref,
    ends_row_ref,
    *refs,
):
    (
        output_ref,
        residual_grad_ref,
        second_ref,
        hidden_ref,
        hidden_grad_ref,
        context_ref,
        attended_grad_ref,
        numer_grad_ref,
        denom_grad_ref,
        vectors_ref,
        bias_grad_ref,
        end_ref,
        state,
        total,
        ups,
        downs,
        biases,
    ) = refs[-17:]
    peers = refs[:-17]
    b = pl.program_id(0)
    shards = ups.shape[0]
    depth = ups.shape[1]

    @pl.when(b == 0)
    def _():
        state[...] = jnp.zeros_like(state)
        total[...] = jnp.zeros_like(total)
        vectors_ref[...] = jnp.zeros_like(vectors_ref)
        bias_grad_ref[...] = jnp.zeros_like(bias_grad_ref)
        ups[0] = up_ref[...]
        downs[0] = down_ref[...]
        biases[0:1, :] = up_bias_ref[...].astype(F32)
        odd = odd_ref[...] != 0
        for j in range(1, shards):
            half_ref, other_ref = peers[2 * j - 2 : 2 * j]
            mine, other = half_ref[:depth], other_ref[:depth]
            ups[j] = jnp.where(odd, other, mine)
            downs[j] = jnp.where(odd, mine, other)
            biases[j : j + 1, :] = half_ref[depth : depth + 1].astype(F32)

    ends_row = ends_row_ref[...]
    own = first_ref[0]
    seg_c = seg_col(ends_row, own + b * CHUNK, CHUNK)
    cont = (seg_c == seg_at(ends_row, own)).astype(F32) * not_open(ends_row, own)
    cont_low = cont.astype(BF)
    diagonal = block_diagonal()
    query = query_ref[...]
    numer, denom = [], []
    for p in range(PAIRS):
        s = pair_slice(p)
        packed = prior_ref[p * HEAD_DIM : (p + 1) * HEAD_DIM, :]
        row = prior_ref[PACK + p : PACK + p + 1, :]
        before = jnp.concatenate(
            [unpack_pair(packed, diagonal), column_of(row) * diagonal], axis=1
        ).astype(BF)
        both = dot(query[:, s] * cont_low, before)
        numer.append(both[:, :LANES])
        denom.append(both[:, LANES:])
    numer = num_ref[...] + jnp.concatenate(numer, axis=1)
    inv_den = 1.0 / (den_ref[...] + jnp.concatenate(denom, axis=1) + SCORE_EPS)
    context = numer * inv_den
    context_low = context.astype(BF)
    context_ref[...] = context_low
    residual = x_ref[...].astype(F32) + dot(context_low, out_w_ref[...])
    gain = gain_ref[...]
    normed, scaled, inv_std = normalize(residual, gain, shift_ref[...])
    second = normed.astype(BF)
    second_ref[...] = second
    g = g_ref[...]
    g_wide = g.astype(F32)
    fed = jnp.zeros((CHUNK, WIDTH), F32)
    second_grad = jnp.zeros((CHUNK, WIDTH), F32)
    for j in range(shards):
        hidden_in = dot(second, ups[j]) + biases[j : j + 1, :]
        phi, bell = normal_parts(hidden_in)
        hidden = (hidden_in * phi).astype(BF)
        hidden_ref[j] = hidden
        fed = fed + dot(hidden, downs[j])
        slope = phi + hidden_in * bell * 0.3989422804014327
        hidden_grad = (dot_t(g, downs[j]) * slope).astype(BF)
        hidden_grad_ref[j] = hidden_grad
        bias_grad_ref[j : j + 1, :] += jnp.sum(hidden_grad.astype(F32), axis=0, keepdims=True)
        second_grad = second_grad + dot_t(hidden_grad, ups[j])
    output_ref[...] = (residual + fed + down_bias_ref[...]).astype(BF)
    vectors_ref[0:1, :] += jnp.sum(second_grad * scaled, axis=0, keepdims=True)
    vectors_ref[1:2, :] += jnp.sum(second_grad, axis=0, keepdims=True)
    vectors_ref[2:3, :] += jnp.sum(g_wide, axis=0, keepdims=True)
    residual_grad = g_wide + normalize_back(second_grad, scaled, inv_std, gain)
    residual_grad_ref[...] = residual_grad
    attended_grad = residual_grad.astype(BF)
    attended_grad_ref[...] = attended_grad
    context_grad = dot_t(attended_grad, out_w_ref[...]).astype(BF).astype(F32)
    numer_grad = (context_grad * inv_den).astype(BF)
    numer_grad_ref[...] = numer_grad
    denom_grad = -head_sums(context_grad * context) * inv_den
    denom_grad_ref[...] = denom_grad
    reach = query * cont_low
    for p in range(PAIRS):
        s = pair_slice(p)
        state[p] += pack_pair(t_dot(reach[:, s], numer_grad[:, s]))
    total[0:1, :] += jnp.sum(reach.astype(F32) * denom_grad, axis=0, keepdims=True)

    @pl.when(b == pl.num_programs(0) - 1)
    def _():
        end_ref[...] = total_rows(
            jnp.concatenate([state[p] for p in range(PAIRS)], axis=0), total[0:1, :]
        ).astype(BF)


def backward_kernel(
    pairs,
    first_ref,
    feat_ref,
    numer_grad_ref,
    denom_grad_ref,
    states_ref,
    totals_ref,
    prior_ref,
    ends_row_ref,
    ends_col_ref,
    grads_ref,
    state,
    total,
):
    step = pl.program_id(0)
    b = pl.num_programs(0) - 1 - step

    @pl.when(step == 0)
    def _():
        state[...] = jnp.zeros_like(state)
        total[...] = jnp.zeros_like(total)

    own = first_ref[0]
    first = own + b * CHUNK
    ends_row = ends_row_ref[...]
    seg_c = seg_col(ends_row, first, CHUNK)
    seg_r = seg_row(ends_col_ref[...], first, CHUNK)
    seg_first = seg_r[:, :1]
    seg_last = seg_r[:, CHUNK - 1 :]
    flow = not_open(ends_row, first)
    carried = (seg_c == seg_first).astype(F32) * flow
    ending = (seg_c == seg_last).astype(F32)
    keep = (seg_first == seg_last).astype(F32) * flow
    prior = (seg_first == seg_at(ends_row, own)).astype(F32) * not_open(ends_row, own)
    square = (CHUNK, CHUNK)
    allowed = jnp.where(
        (iota(square, 1) <= iota(square, 0)) & (seg_c == seg_r), 1.0, 0.0
    )
    diagonal = block_diagonal()
    masks = lane_masks(BF)
    carried_low = carried.astype(BF)
    lane = iota((1, LANES), 1)
    upper = lane % HEAD_DIM < HEAD_DIM // 2
    for p in pairs:
        s = pair_slice(p)
        q = feat_ref[:, s]
        k = feat_ref[:, WIDTH + p * LANES : WIDTH + (p + 1) * LANES]
        v = feat_ref[:, 2 * WIDTH + p * LANES : 2 * WIDTH + (p + 1) * LANES]
        at = p - pairs[0]
        ng = numer_grad_ref[:, s]
        dg = denom_grad_ref[:, s]
        dg_high = dg.astype(BF).astype(F32)
        dg_parts = jnp.where(upper, dg_high, dg - dg_high).astype(BF)
        left = jnp.concatenate([ng, dg_parts], axis=1)
        pair_grads, keys, key_grad, value_grad = [], [], 0.0, 0.0
        for h, m in enumerate(masks):
            k_own = k * m
            keys.append(k_own)
            weights = (dot_t(q, k_own) * allowed).astype(BF)
            pick = (lane == h * HEAD_DIM) | (lane == h * HEAD_DIM + HEAD_DIM // 2)
            pick = jnp.where(pick, 1.0, 0.0).astype(BF)
            right = jnp.concatenate(
                [v * m, jnp.broadcast_to(pick, (CHUNK, LANES))], axis=1
            )
            pair_grad = (dot_t(left, right) * allowed).astype(BF)
            pair_grads.append(pair_grad)
            key_grad = key_grad + t_dot(pair_grad, q * m)
            value_grad = value_grad + t_dot(weights, ng * m)
        rows = slice(p * HEAD_DIM, (p + 1) * HEAD_DIM)
        packed = states_ref[0, rows, :] + prior * prior_ref[rows, :]
        row = totals_ref[0, 0:1, s] + prior * prior_ref[PACK + p : PACK + p + 1, :]
        before = unpack_pair(packed, diagonal).astype(BF)
        query_grad = dot(
            jnp.concatenate(pair_grads, axis=1), jnp.concatenate(keys, axis=0)
        ) + carried * (dot_t(ng, before) + dg * row)
        after = state[p]
        after_row = total[0:1, s]
        after_low = unpack_pair(after, diagonal).astype(BF)
        key_grad = key_grad + ending * (dot_t(v, after_low) + after_row)
        value_grad = value_grad + ending * dot(k, after_low)
        grads_ref[:, pair_slice(3 * at)] = query_grad
        grads_ref[:, pair_slice(3 * at + 1)] = key_grad
        grads_ref[:, pair_slice(3 * at + 2)] = value_grad
        reach = q * carried_low
        state[p] = keep * after + pack_pair(t_dot(reach, ng))
        total[0:1, s] = keep * after_row + jnp.sum(
            reach.astype(F32) * dg, axis=0, keepdims=True
        )


def last_kernel(
    first_ref,
    x_ref,
    feat_ref,
    later_ref,
    w_ref,
    gain_ref,
    shift_ref,
    residual_grad_ref,
    ends_row_ref,
    *refs,
):
    grads, (projected_grad_ref, input_grad_ref, vectors_ref) = refs[:-3], refs[-3:]
    per_call = PAIRS // len(grads)
    b = pl.program_id(0)

    @pl.when(b == 0)
    def _():
        vectors_ref[...] = jnp.zeros_like(vectors_ref)

    ends_row = ends_row_ref[...]
    own = first_ref[0]
    span = pl.num_programs(0) * CHUNK
    seg_c = seg_col(ends_row, own + b * CHUNK, CHUNK)
    reached = (seg_c == seg_at(ends_row, own + span - 1)).astype(F32)
    diagonal = block_diagonal()
    for p in range(PAIRS):
        sq = pair_slice(p)
        sk = pair_slice(PAIRS + p)
        sv = pair_slice(2 * PAIRS + p)
        after = unpack_pair(
            later_ref[p * HEAD_DIM : (p + 1) * HEAD_DIM, :], diagonal
        ).astype(BF)
        after_row = later_ref[PACK + p : PACK + p + 1, :]
        k = feat_ref[:, sk]
        grads_ref, at = grads[p // per_call], 3 * (p % per_call)
        key_grad = grads_ref[:, pair_slice(at + 1)] + reached * (dot_t(feat_ref[:, sv], after) + after_row)
        value_grad = grads_ref[:, pair_slice(at + 2)] + reached * dot(k, after)
        q_slope = jnp.minimum(feat_ref[:, sq].astype(F32), 1.0)
        k_slope = jnp.minimum(k.astype(F32), 1.0)
        projected_grad_ref[:, sq] = (grads_ref[:, pair_slice(at)] * q_slope).astype(BF)
        projected_grad_ref[:, sk] = (key_grad * k_slope).astype(BF)
        projected_grad_ref[:, sv] = value_grad.astype(BF)
    first_grad = dot_t(projected_grad_ref[...], w_ref[...])
    gain = gain_ref[...]
    _, scaled, inv_std = normalize(x_ref[...].astype(F32), gain, shift_ref[...])
    vectors_ref[0:1, :] += jnp.sum(first_grad * scaled, axis=0, keepdims=True)
    vectors_ref[1:2, :] += jnp.sum(first_grad, axis=0, keepdims=True)
    input_grad_ref[...] = (
        residual_grad_ref[...] + normalize_back(first_grad, scaled, inv_std, gain)
    ).astype(BF)


def call(kernel, steps, ins, outs, scratch=(), reverse=False, cost=10, name=None):
    def spec(shape, dim, size):
        if dim is None:
            return pl.BlockSpec(shape, lambda i: (0,) * len(shape))
        block = shape[:dim] + (size,) + shape[dim + 1 :]

        def place(i):
            at = steps - 1 - i if reverse else i
            return tuple(at if d == dim else 0 for d in range(len(shape)))

        return pl.BlockSpec(block, place)

    in_specs = []
    for array, dim in ins:
        if dim == "scalar":
            in_specs.append(pl.BlockSpec(memory_space=pltpu.SMEM))
        else:
            size = None if dim is None else array.shape[dim] // steps
            in_specs.append(spec(array.shape, dim, size))
    out_specs = [
        spec(shape, dim, None if dim is None else shape[dim] // steps) for shape, _, dim in outs
    ]
    return pl.pallas_call(
        kernel,
        grid=(steps,),
        in_specs=in_specs,
        out_specs=out_specs,
        out_shape=[jax.ShapeDtypeStruct(shape, dtype) for shape, dtype, _ in outs],
        scratch_shapes=list(scratch),
        compiler_params=pltpu.CompilerParams(vmem_limit_bytes=56 * 1024 * 1024),
        name=name or kernel.__name__,
        cost_estimate=pl.CostEstimate(
            flops=int(cost * 1e9), transcendentals=0, bytes_accessed=int(cost * 3e6)
        ),
    )(*[array for array, _ in ins])


def shift(array, axis, by):
    n = lax.axis_size(axis)
    return lax.ppermute(array, axis, [(i, (i + by) % n) for i in range(n)])


def swap(array, axis, bit):
    n = lax.axis_size(axis)
    return lax.ppermute(array, axis, [(i, i ^ bit) for i in range(n)])


def bits_of(n):
    return [1 << i for i in range(n.bit_length() - 1)]


def bit_set(axis, bit):
    return (lax.axis_index(axis) // bit) % 2


def half(array, dim, which):
    size = array.shape[dim] // 2
    return lax.dynamic_slice_in_dim(array, which * size, size, dim)


def send_parts(parts, dim, move):
    moved = move(jnp.concatenate(parts, axis=dim))
    cuts, at = [], 0
    for part in parts:
        cuts.append(lax.slice_in_dim(moved, at, at + part.shape[dim], axis=dim))
        at += part.shape[dim]
    return cuts


def halve(array, bit, dim):
    mine = bit_set("dp", bit)
    return half(array, dim, mine), half(array, dim, 1 - mine).astype(BF)


def join_halves(array, other, bit, dim):
    return jnp.where(
        bit_set("dp", bit) == 0,
        jnp.concatenate([array, other], axis=dim),
        jnp.concatenate([other, array], axis=dim),
    )


def reduce_pair(parts, dim, bits, piece, everywhere):
    n_mp, z_at = lax.axis_size("mp"), lax.axis_index("mp")
    join = parts[0].ndim - 1
    for step in range(len(bits[0])):
        both = [halve(p, b[step], dim) for p, b in zip(parts, bits)]
        sent = [pair[1] for pair in both]
        if bits[0][step] == bits[1][step]:
            got = send_parts(sent, join, lambda a: swap(a, "dp", bits[0][step]))
        else:
            got = [swap(a, "dp", b[step]) for a, b in zip(sent, bits)]
        parts = [pair[0] + a.astype(F32) for pair, a in zip(both, got)]
    own = [piece(p, 0) for p in parts]
    last = own[0].ndim - 1
    got = [
        send_parts([piece(p, k).astype(BF) for p in parts], last, lambda a, k=k: shift(a, "mp", -k))
        for k in range(1, n_mp)
    ]
    for pair in got:
        own = [o + a.astype(F32) for o, a in zip(own, pair)]
    own = [o.astype(BF) for o in own]
    if everywhere:
        wide = jnp.concatenate(own, axis=1)
        whole = lax.dynamic_update_slice_in_dim(
            jnp.zeros((n_mp,) + wide.shape, BF), wide[None], z_at, 0
        )
        for k in range(1, n_mp):
            whole = lax.dynamic_update_slice_in_dim(
                whole, shift(wide, "mp", k)[None], (z_at - k) % n_mp, 0
            )
        whole = whole.reshape(n_mp * wide.shape[0], wide.shape[1])
        own = [whole[:, : own[0].shape[1]], whole[:, own[0].shape[1] :]]
    for step in reversed(range(len(bits[0]))):
        if bits[0][step] == bits[1][step]:
            got = send_parts(own, 1, lambda a: swap(a, "dp", bits[0][step]))
        else:
            got = [swap(a, "dp", b[step]) for a, b in zip(own, bits)]
        own = [join_halves(o, a, b[step], 0) for o, a, b in zip(own, got, bits)]
    return [o.astype(F32) for o in own]


def orders(n):
    bits = bits_of(n)
    if len(bits) < 3:
        return bits, bits
    return bits, bits[:1] + bits[2:] + bits[1:2]


def local(
    tokens,
    qkv_weight,
    out_weight,
    norm1_gain,
    norm1_shift,
    norm2_gain,
    norm2_shift,
    up_weight,
    up_bias,
    down_weight,
    down_bias,
    lengths,
    cotangent,
):
    rows, width = tokens.shape
    steps = rows // CHUNK
    n_dp, n_mp = lax.axis_size("dp"), lax.axis_size("mp")
    g_at, z_at = lax.axis_index("dp"), lax.axis_index("mp")
    me = g_at * n_mp + z_at
    first = (me * rows).astype(jnp.int32).reshape(1)
    n_seq = lengths.shape[0]
    order = jnp.arange(n_seq)
    ends = jnp.sum(jnp.where(order[:, None] >= order[None, :], lengths[None, :], 0), axis=1)
    ends_row = ends.reshape(1, n_seq).astype(jnp.int32)
    ends_col = ends.reshape(n_seq, 1).astype(jnp.int32)
    rows_of = lambda v: v.reshape(1, -1)

    shard = up_weight.shape[1]
    odd = bit_set("dp", 1)
    sent = jnp.concatenate(
        [
            jnp.where(odd == 0, up_weight, down_weight),
            jnp.broadcast_to(up_bias[None], (16, shard)),
        ]
    )
    halves = [shift(sent, "mp", k) for k in range(1, n_mp)]
    others = [swap(h, "dp", 1) for h in halves]
    peers = [(a, None) for pair in zip(halves, others) for a in pair]

    scratch = [pltpu.VMEM((PAIRS, HEAD_DIM, LANES), F32), pltpu.VMEM((8, WIDTH), F32)]
    gain1, shift1 = rows_of(norm1_gain), rows_of(norm1_shift)
    normed_low, feat, numer, denom, states, totals, end_state = call(
        forward_kernel,
        steps,
        [
            (first, "scalar"),
            (tokens, 0),
            (qkv_weight, None),
            (gain1, None),
            (shift1, None),
            (ends_row, None),
            (ends_col, None),
        ],
        [
            ((rows, width), BF, 0),
            ((rows, 3 * width), BF, 0),
            ((rows, width), F32, 0),
            ((rows, width), F32, 0),
            ((steps, PACK, LANES), F32, 0),
            ((steps, 8, width), F32, 0),
            ((PAYLOAD, LANES), BF, None),
        ],
        scratch,
    )

    def sum_states(payload, ok):
        column = lax.all_gather(payload, "dp").astype(F32)
        senders = jnp.arange(n_dp, dtype=jnp.int32) * n_mp + z_at
        takers = [g_at * n_mp + (z_at + k) % n_mp for k in range(n_mp)]
        weights = jnp.stack([ok(senders, t) for t in takers]).astype(F32)
        sums = jnp.sum(weights[:, :, None, None] * column[None], axis=1)
        out = sums[0]
        for k in range(1, n_mp):
            out = out + shift(sums[k].astype(BF), "mp", k).astype(F32)
        return out

    def segment_of(place):
        return jnp.sum((ends <= place[..., None]).astype(jnp.int32), axis=-1)

    def before(sender, taker):
        same = segment_of(sender * rows + (rows - 1)) == segment_of(taker * rows)
        return (sender < taker) & same

    def after(sender, taker):
        same = segment_of(sender * rows) == segment_of(taker * rows + (rows - 1))
        return (sender > taker) & same

    prior = sum_states(end_state, before)

    gain2, shift2 = rows_of(norm2_gain), rows_of(norm2_shift)
    (
        output,
        residual_grad,
        second,
        hidden,
        hidden_grad,
        context_low,
        attended_grad,
        numer_grad,
        denom_grad,
        vectors2,
        bias_grad,
        end_grad,
    ) = call(
        middle_kernel,
        steps,
        [
            (first, "scalar"),
            (tokens, 0),
            (feat[:, :width], 0),
            (numer, 0),
            (denom, 0),
            (prior, None),
            (out_weight, None),
            (gain2, None),
            (shift2, None),
            (up_weight, None),
            (rows_of(up_bias), None),
            (down_weight, None),
            (rows_of(down_bias), None),
            (jnp.broadcast_to(odd, (1, shard)).astype(jnp.int32), None),
            (cotangent, 0),
            (ends_row, None),
            *peers,
        ],
        [
            ((rows, width), BF, 0),
            ((rows, width), F32, 0),
            ((rows, width), BF, 0),
            ((n_mp, rows, shard), BF, 1),
            ((n_mp, rows, shard), BF, 1),
            ((rows, width), BF, 0),
            ((rows, width), BF, 0),
            ((rows, width), BF, 0),
            ((rows, width), F32, 0),
            ((8, width), F32, None),
            ((n_mp, shard), F32, None),
            ((PAYLOAD, LANES), BF, None),
        ],
        scratch
        + [
            pltpu.VMEM((n_mp, width, shard), BF),
            pltpu.VMEM((n_mp, shard, width), BF),
            pltpu.VMEM((8, shard), F32),
        ],
        cost=29,
    )
    later = sum_states(end_grad, after)

    up_pieces = jnp.einsum("td,jtf->jdf", second, hidden_grad, preferred_element_type=F32)
    down_pieces = jnp.einsum("jtf,td->jfd", hidden, cotangent, preferred_element_type=F32)
    order_a, order_b = orders(n_dp)
    grad_up, grad_down = reduce_pair(
        (up_pieces, down_pieces), 1, (order_a, order_b), lambda part, k: part[k], False
    )

    per_call = PAIRS // BACK_CALLS
    grads = [
        call(
            functools.partial(backward_kernel, tuple(range(c * per_call, (c + 1) * per_call))),
            steps,
            [
                (first, "scalar"),
                (feat, 0),
                (numer_grad, 0),
                (denom_grad, 0),
                (states, 0),
                (totals, 0),
                (prior, None),
                (ends_row, None),
                (ends_col, None),
            ],
            [((rows, 3 * per_call * LANES), F32, 0)],
            scratch,
            reverse=True,
            cost=16 / BACK_CALLS,
            name=f"backward_{c}",
        )[0]
        for c in range(BACK_CALLS)
    ]
    projected_grad, input_grad, vectors1 = call(
        last_kernel,
        steps,
        [
            (first, "scalar"),
            (tokens, 0),
            (feat, 0),
            (later, None),
            (qkv_weight, None),
            (gain1, None),
            (shift1, None),
            (residual_grad, 0),
            (ends_row, None),
            *[(part, 0) for part in grads],
        ],
        [
            ((rows, 3 * width), BF, 0),
            ((rows, width), BF, 0),
            ((8, width), F32, None),
        ],
    )
    grad_qkv = jnp.einsum("td,tk->dk", normed_low, projected_grad, preferred_element_type=F32)
    grad_out = jnp.einsum("ti,to->io", context_low, attended_grad, preferred_element_type=F32)

    bias_here = jnp.stack(
        [lax.dynamic_index_in_dim(bias_grad, (z_at - j) % n_mp, 0, False) for j in range(n_mp)]
    )
    small = jnp.concatenate([vectors1[:2], vectors2[:3], bias_here], axis=0)
    small = jnp.pad(small, ((0, LANES - small.shape[0]), (0, 0))).T
    parts = (grad_qkv[:, : 2 * width], jnp.concatenate([grad_qkv[:, 2 * width :], grad_out, small], 1))

    def rows_for(part, k):
        size = part.shape[0] // n_mp
        return lax.dynamic_slice_in_dim(part, ((z_at - k) % n_mp) * size, size, 0)

    grad_a, grad_b = reduce_pair(parts, 0, (order_a, order_b), rows_for, True)
    vec = grad_b[:, 2 * width : 2 * width + 5 + n_mp].T

    return (
        output,
        input_grad,
        jnp.concatenate([grad_a, grad_b[:, :width]], axis=1),
        grad_b[:, width : 2 * width],
        vec[0],
        vec[1],
        vec[2],
        vec[3],
        grad_up,
        lax.dynamic_index_in_dim(vec, 5 + z_at, 0, False),
        grad_down,
        vec[4],
    )


def solution(mesh):
    in_specs = (
        P(("dp", "mp"), None),
        P(),
        P(),
        P(),
        P(),
        P(),
        P(),
        P(None, "mp"),
        P("mp"),
        P("mp", None),
        P(),
        P(),
        P(("dp", "mp"), None),
    )
    out_specs = (
        P(("dp", "mp"), None),
        P(("dp", "mp"), None),
        P(),
        P(),
        P(),
        P(),
        P(),
        P(),
        P(None, "mp"),
        P("mp"),
        P("mp", None),
        P(),
    )
    return jax.shard_map(local, mesh=mesh, in_specs=in_specs, out_specs=out_specs, check_vma=False)
```
